256 devices in a mesh: tensor: 4 (over x), shard: 64 (over z, y, core).
Axes of the slice: x: 4, y: 4, z: 8, core: 2. Of those that a mesh axis runs over, the one named last changes fastest.
Arguments:
- proj_grads: bfloat16 [128, 2, 1152, 1024], P('shard', None, None, 'tensor'), may hold values from -60 to 60
- kv_grads: bfloat16 [512, 1152, 512], P(('tensor', 'shard')), may hold values from -60 to 60
- gain_grads: bfloat16 [512, 2, 256], P(('tensor', 'shard')), may hold values from -60 to 60
- proj_master: float32 [2, 1152, 1024], P(None, 'shard', 'tensor'), may hold values from -0.3125 to 0.3125
- proj_m: float32 [2, 1152, 1024], P(None, 'shard', 'tensor'), may hold values from -1.5 to 1.5
- proj_v: float32 [2, 1152, 1024], P(None, 'shard', 'tensor'), may hold values from 0.02 to 0.5
- kv_master: float32 [1152, 512], P('shard', 'tensor'), may hold values from -0.3125 to 0.3125
- kv_m: float32 [1152, 512], P('shard', 'tensor'), may hold values from -1.5 to 1.5
- kv_v: float32 [1152, 512], P('shard', 'tensor'), may hold values from 0.02 to 0.5
- gains: float32 [2, 256], replicated, may hold values from 0.1 to 1.9
- gains_m: float32 [2, 256], replicated, may hold values from -6 to 6
- gains_v: float32 [2, 256], replicated, may hold values from 0.25 to 4
Outputs:
- proj_master_new: float32 [2, 1152, 1024], P(None, 'shard', 'tensor')
- proj_m_new: float32 [2, 1152, 1024], P(None, 'shard', 'tensor')
- proj_v_new: float32 [2, 1152, 1024], P(None, 'shard', 'tensor')
- proj_weights: bfloat16 [2, 1152, 1024], P(None, None, 'tensor')
- kv_master_new: float32 [1152, 512], P('shard', 'tensor')
- kv_m_new: float32 [1152, 512], P('shard', 'tensor')
- kv_v_new: float32 [1152, 512], P('shard', 'tensor')
- kv_weights: bfloat16 [1152, 512], replicated
- gains_new: float32 [2, 256], replicated
- gains_m_new: float32 [2, 256], replicated
- gains_v_new: float32 [2, 256], replicated
The draws below stay inside these ranges and needn't reach their ends.
All inputs are finite; a program needn't handle non-finite values.
Results may differ from the reference program's by a relative error of at most 0.0004.
Values may be sent and summed in bfloat16 or wider, within the bound.
A program may use at most 64 MiB of HBM per device.

```python
import math
import jax
import jax.numpy as jnp
from jax import lax

D = 1152
HD = 256
QW = 1024
KVW = 512
PARAMS = 2949632
GRAD_ROWS = 128
KV_ROWS = 512


def rough_grads(key, array_shape, row_dim):
    key_noise = jax.random.fold_in(key, 0)
    row_count = array_shape[row_dim]
    scale_shape = [1] * len(array_shape)
    scale_shape[row_dim] = row_count
    row_scale = (1.0 + 2.0 * jnp.arange(row_count, dtype=jnp.float32) / max(row_count - 1, 1)).reshape(scale_shape)
    col_count = array_shape[-1]
    col_shape = [1] * len(array_shape)
    col_shape[-1] = col_count
    col_scale = (1.0 + 2.0 * jnp.arange(col_count, dtype=jnp.float32) / max(col_count - 1, 1)).reshape(col_shape)
    fresh_noise = jnp.clip(jax.random.normal(key_noise, array_shape, jnp.float32), -5.0, 5.0)
    values = fresh_noise * row_scale * col_scale
    return values.astype(jnp.bfloat16)


def draw_proj_grads(key, part):
    return rough_grads(jax.random.fold_in(key, 11), (GRAD_ROWS, 2, D, QW), 2)


def draw_kv_grads(key, part):
    return rough_grads(jax.random.fold_in(key, 23), (KV_ROWS, D, KVW), 1)


def draw_gain_grads(key, part):
    return rough_grads(jax.random.fold_in(key, 37), (KV_ROWS, 2, HD), 0)


def levels(own_key, extent, cuts, least, largest):
    level, own = 1.0, jax.random.fold_in(own_key, 6)
    for position, blocks in cuts:
        heights = jnp.exp(jax.random.uniform(jax.random.fold_in(own, position), (blocks,), jnp.float32, least / len(cuts), largest / len(cuts)))
        level = level * jnp.repeat(heights, extent[position] // blocks).reshape([-1 if axis == position else 1 for axis in range(len(extent))])
    return level


def scatter_about(rng, shape, scale, reach, cuts=(), kind=jnp.bfloat16):
    drawn = jax.random.normal(rng, shape, jnp.float32) * scale
    if len(cuts) > 0:
        drawn = levels(rng, shape, cuts, -0.22, 0.18) * drawn
    return jnp.clip(drawn, min=-reach, max=reach).astype(kind)


def setup_inputs(seed: int = 0) -> dict:
    key_list = jax.random.split(jax.random.key(seed), 13)
    proj_grads = draw_proj_grads(jax.random.fold_in(key_list[12], 71), 0)
    kv_grads = draw_kv_grads(jax.random.fold_in(key_list[12], 71), 0)
    gain_grads = draw_gain_grads(jax.random.fold_in(key_list[12], 71), 0)
    proj_master = scatter_about(key_list[3], (2, D, QW), 0.02, 0.3125, ((1, 64), (2, 4)), jnp.float32)
    proj_m = scatter_about(key_list[4], (2, D, QW), 0.1, 1.5, ((1, 64), (2, 4)), jnp.float32)
    proj_v = jnp.clip(jnp.exp(math.log(0.5) - 3.218876 * jax.random.uniform(key_list[5], (2, D, QW), jnp.float32) ** levels(key_list[5], (2, D, QW), ((1, 64), (2, 4)), -0.2, 0.2)), 0.02, 0.5)
    kv_master = scatter_about(key_list[6], (D, KVW), 0.02, 0.3125, ((0, 64), (1, 4)), jnp.float32)
    kv_m = scatter_about(key_list[7], (D, KVW), 0.1, 1.5, ((0, 64), (1, 4)), jnp.float32)
    kv_v = jnp.clip(jnp.exp(math.log(0.5) - 3.218876 * jax.random.uniform(key_list[8], (D, KVW), jnp.float32) ** levels(key_list[8], (D, KVW), ((0, 64), (1, 4)), -0.2, 0.2)), 0.02, 0.5)
    gains = jnp.clip(1.0 + 0.18 * jax.random.normal(key_list[9], (2, HD), jnp.float32), 0.1, 1.9)
    gains_m = scatter_about(key_list[10], (2, HD), 1.0, 6.0, (), jnp.float32)
    gains_v = jnp.clip(jnp.exp(jax.random.uniform(key_list[11], (2, HD), jnp.float32, math.log(0.25), math.log(4.0))), 0.25, 4.0)
    return {"proj_grads": proj_grads, "kv_grads": kv_grads, "gain_grads": gain_grads, "proj_master": proj_master, "proj_m": proj_m, "proj_v": proj_v, "kv_master": kv_master, "kv_m": kv_m, "kv_v": kv_v, "gains": gains, "gains_m": gains_m, "gains_v": gains_v}


beta_one = 0.9
beta_two = 0.95
learn_rate = 0.01
decay_rate = 0.1
epsilon = 1e-08
step_count = 10

def adamw_step(master, moment, second, update_grad, decay):
    moment_new = beta_one * moment + (1.0 - beta_one) * update_grad
    second_new = beta_two * second + (1.0 - beta_two) * update_grad * update_grad
    first_hat = moment_new / (1.0 - beta_one ** step_count)
    second_hat = second_new / (1.0 - beta_two ** step_count)
    master_new = master - learn_rate * (first_hat / (jnp.sqrt(second_hat) + epsilon) + decay * master)
    return (master_new, moment_new, second_new)

def reference(proj_grads, kv_grads, gain_grads, proj_master, proj_m, proj_v, kv_master, kv_m, kv_v, gains, gains_m, gains_v):
    proj_sum = lax.optimization_barrier(jnp.sum(proj_grads, axis=0, dtype=jnp.float32))
    kv_sum = lax.optimization_barrier(jnp.sum(kv_grads, axis=0, dtype=jnp.float32))
    gain_sum = lax.optimization_barrier(jnp.sum(gain_grads, axis=0, dtype=jnp.float32))
    norm_square = jnp.sum(proj_sum * proj_sum) + jnp.sum(kv_sum * kv_sum) + jnp.sum(gain_sum * gain_sum)
    clip_factor = jnp.minimum(1.0, math.sqrt(PARAMS) / jnp.sqrt(norm_square))
    proj_new, proj_m_new, proj_v_new = adamw_step(proj_master, proj_m, proj_v, clip_factor * proj_sum, decay_rate)
    kv_new, kv_m_new, kv_v_new = adamw_step(kv_master, kv_m, kv_v, clip_factor * kv_sum, decay_rate)
    gains_new, gains_m_new, gains_v_new = adamw_step(gains, gains_m, gains_v, clip_factor * gain_sum, 0.0)
    return (proj_new, proj_m_new, proj_v_new, proj_new.astype(jnp.bfloat16), kv_new, kv_m_new, kv_v_new, kv_new.astype(jnp.bfloat16), gains_new, gains_m_new, gains_v_new)
```

```python
import math

import jax
import jax.numpy as jnp
from jax import lax
from jax.experimental import pallas as pl
from jax.experimental.pallas import tpu as pltpu
from jax.sharding import PartitionSpec as P

PARAMS = 2949632
MESH = pl.DeviceIdType.MESH
F32, BF16 = jnp.float32, jnp.bfloat16

NZ, NY, NC, NX = 8, 4, 2, 4
R = 18
ZR = NY * NC * R
LANES = 128

beta_one = 0.9
beta_two = 0.95
learn_rate = 0.01
decay_rate = 0.1
epsilon = 1e-08
step_count = 10


def adamw_step(master, moment, second, update_grad, decay):
    moment_new = beta_one * moment + (1.0 - beta_one) * update_grad
    second_new = beta_two * second + (1.0 - beta_two) * update_grad * update_grad
    first_hat = moment_new / (1.0 - beta_one**step_count)
    second_hat = second_new / (1.0 - beta_two**step_count)
    master_new = master - learn_rate * (
        first_hat / (jnp.sqrt(second_hat) + epsilon) + decay * master
    )
    return (master_new, moment_new, second_new)


def clip_of(tile):
    row = lax.broadcasted_iota(jnp.int32, tile.shape, 0)
    terms = jnp.where(row < 4, tile * tile, jnp.where(row == 4, tile, 0.0))
    norm_square = jnp.sum(jnp.sum(terms, axis=0, keepdims=True), axis=1, keepdims=True)
    return jnp.minimum(1.0, math.sqrt(PARAMS) / jnp.sqrt(norm_square))


class Links:
    def __init__(self, send_sems, recv_sems, local_sems):
        self.send_sems, self.recv_sems, self.local_sems = send_sems, recv_sems, local_sems
        self.started, self.locals = [], 0

    def send(self, src, dst, device):
        number = len(self.started)
        copy = pltpu.make_async_remote_copy(
            src_ref=src,
            dst_ref=dst,
            send_sem=self.send_sems.at[number],
            recv_sem=self.recv_sems.at[number],
            device_id=device,
            device_id_type=MESH,
        )
        copy.start()
        self.started.append(copy)
        return copy

    def local(self, src, dst):
        copy = pltpu.make_async_copy(src, dst, self.local_sems.at[self.locals])
        self.locals += 1
        copy.start()
        return copy

    def finish(self):
        for copy in self.started:
            copy.wait_send()


N_COPIES = 176


def scatter_ring(links, n, pos, device, view, slot):
    half = n // 2
    copies = {}

    def step(way, part, d):
        dest = lax.rem(pos + way * d + n, n)
        copies[way, part, d] = links.send(view(dest, part), slot(way, part, d), device(lax.rem(pos + way + n, n)))

    def take(way, part, d):
        copies[way, part, d].wait_recv()
        dest = lax.rem(pos + way * (d - 1) + n, n)
        ref, got = view(dest, part), slot(way, part, d)
        ref[...] = ref[...] + got[...]

    for way in (1, -1):
        step(way, 0 if way == 1 else 1, half)
    if half > 1:
        for way in (1, -1):
            step(way, 1 if way == 1 else 0, half - 1)
    for d in range(half - 1, 0, -1):
        yield
        for way in (1, -1):
            lead = 0 if way == 1 else 1
            take(way, lead, d + 1)
            step(way, lead, d)
        if d < half - 1:
            for way in (1, -1):
                other = 1 if way == 1 else 0
                take(way, other, d + 1)
                step(way, other, d)
    yield
    for way in (1, -1):
        for part in (0, 1):
            if (way, part, 1) in copies:
                take(way, part, 1)


def run(*generators):
    waiting = list(generators)
    while waiting:
        waiting = [g for g in waiting if next(g, "end") != "end"]


def step_kernel(
    pg, kg, gg, p_master, p_m, p_v, k_master, k_m, k_v,
    psum_o, ksum_o, tile_o, pw_o, kw_o,
    pgv, kgv, PA, PB, KK, RA, RB, RK, T,
    rAy, rBz, rKx, rAz0, rAz1, rBy, rKy, K3, rKz0, rKz1,
    tc, tx, ty, tz, S72, W96, G, FK, T5,
    send_sems, recv_sems, local_sems,
):
    shard, x = lax.axis_index("shard"), lax.axis_index("tensor")
    c = lax.rem(shard, NC)
    y = lax.rem(shard // NC, NY)
    z = shard // (NC * NY)
    oc = 1 - c

    def device(z=z, y=y, c=c, x=x):
        return {"shard": (z * NY + y) * NC + c, "tensor": x}

    links = Links(send_sems, recv_sems, local_sems)
    sibling = device(c=oc)
    others = [sibling]
    others += [device(x=lax.rem(x + d, NX)) for d in range(1, NX)]
    others += [device(y=lax.rem(y + d, NY)) for d in range(1, NY)]
    others += [device(z=lax.rem(z + d, NZ)) for d in range(1, NZ)]

    k_in = links.local(kg, kgv)
    p_in = links.local(pg, pgv)
    barrier = pltpu.get_barrier_semaphore()
    for other in others:
        pl.semaphore_signal(barrier, inc=1, device_id=other, device_id_type=MESH)

    gain = gg[0].astype(F32) + gg[1].astype(F32)
    tc[c] = jnp.zeros((8, LANES), F32)
    for i in range(2):
        for h in range(2):
            tc[c, 2 * i + h : 2 * i + h + 1, :] = gain[i : i + 1, h * LANES : (h + 1) * LANES]

    k_in.wait()
    barrier_done = False
    k_cores = []
    for dx in (2, 1, 3, 0):
        xx = lax.rem(x + dx, NX)
        col = pl.ds(pl.multiple_of(xx * LANES, LANES), LANES)

        @pl.loop(0, 2)
        def _(zh):
            for zl in range(4):
                rows = pl.ds(pl.multiple_of((zh * 4 + zl) * ZR, 16), ZR)
                T[...] = kgv[0, rows, col].astype(F32) + kgv[1, rows, col].astype(F32)
                for k in range(NY * NC):
                    KK[k % NC, xx, k // NC, zh, R * zl : R * zl + R, :] = T[R * k : R * k + R, :]

        if not barrier_done:
            pl.semaphore_wait(barrier, len(others))
            barrier_done = True
        k_cores.append((xx, links.send(KK.at[oc, xx], RK.at[xx], sibling)))

    p_in.wait()
    for p in range(2):

        @pl.loop(0, NZ)
        def _(zz):
            rows = pl.ds(pl.multiple_of(zz * ZR, 16), ZR)
            for h in range(2):
                col = slice(h * LANES, (h + 1) * LANES)
                T[...] = pgv[0, p, rows, col].astype(F32) + pgv[1, p, rows, col].astype(F32)
                for k in range(NY * NC):
                    yy, cc = k // NC, k % NC
                    q = 2 * p + h
                    if q < 2:
                        PA[cc, yy, zz, R * q : R * q + R, :] = T[R * k : R * k + R, :]
                    elif q == 2:
                        PA[cc, yy, zz, 36:40, :] = T[R * k : R * k + 4, :]
                        PB[cc, zz, yy, 0:14, :] = T[R * k + 4 : R * k + R, :]
                    else:
                        PB[cc, zz, yy, 14:32, :] = T[R * k : R * k + R, :]

    b_core = links.send(PB.at[oc], RB, sibling)
    a_core = links.send(PA.at[oc], RA, sibling)

    for xx, copy in k_cores:
        copy.wait_recv()
        KK[c, xx] = KK[c, xx] + RK[xx]
    ring_kx = scatter_ring(
        links, NX, x, lambda i: device(x=i),
        lambda i, part: KK.at[c, i, 2 * part : 2 * part + 2],
        lambda way, part, d: rKx.at[(1 - way) // 2, part, d - 1],
    )
    next(ring_kx)
    b_core.wait_recv()

    @pl.loop(0, NZ)
    def _(zz):
        PB[c, zz] = PB[c, zz] + RB[zz]

    ring_bz = scatter_ring(
        links, NZ, z, lambda i: device(z=i),
        lambda i, part: PB.at[c, i, 2 * part : 2 * part + 2],
        lambda way, part, d: rBz.at[(1 - way) // 2, part, d - 1],
    )
    next(ring_bz)
    a_core.wait_recv()

    @pl.loop(0, NY)
    def _(yy):
        PA[c, yy] = PA[c, yy] + RA[yy]

    ring_ay = scatter_ring(
        links, NY, y, lambda i: device(y=i),
        lambda i, part: PA.at[c, i, 4 * part : 4 * part + 4],
        lambda way, part, d: rAy.at[(1 - way) // 2, part, d - 1],
    )
    next(ring_ay)

    run(ring_ay, ring_bz, ring_kx)

    cut_a, cut_b = (slice(0, 24), slice(24, 40)), (slice(0, 16), slice(16, 32))
    ring_az = scatter_ring(
        links, NZ, z, lambda i: device(z=i),
        lambda i, part: PA.at[c, y, i, cut_a[part]],
        lambda way, part, d: (rAz0, rAz1)[part].at[(1 - way) // 2, d - 1],
    )
    ring_by = scatter_ring(
        links, NY, y, lambda i: device(y=i),
        lambda i, part: PB.at[c, z, i, cut_b[part]],
        lambda way, part, d: rBy.at[(1 - way) // 2, part, d - 1],
    )
    ring_ky = scatter_ring(
        links, NY, y, lambda i: device(y=i),
        lambda i, part: KK.at[c, x, i, part],
        lambda way, part, d: rKy.at[(1 - way) // 2, part, d - 1],
    )
    run(ring_ky, ring_az, ring_by)

    K3[...] = jnp.zeros_like(K3)
    for zz in range(NZ):
        K3[zz, 0:R, :] = KK[c, x, y, zz // 4, R * (zz % 4) : R * (zz % 4) + R, :]
    cut_k = (slice(0, 16), slice(16, 24))
    ring_kz = scatter_ring(
        links, NZ, z, lambda i: device(z=i),
        lambda i, part: K3.at[i, cut_k[part]],
        lambda way, part, d: (rKz0, rKz1)[part].at[(1 - way) // 2, d - 1],
    )
    run(ring_kz)

    S72[0:40, :] = PA[c, y, z]
    S72[40:72, :] = PB[c, z, y]
    p_sum, k_sum = S72[...], K3[z]
    squares = jnp.sum(p_sum * p_sum, axis=0, keepdims=True) + jnp.sum(k_sum * k_sum, axis=0, keepdims=True)
    tc[c, 4:5, :] = squares
    for slots, n, me, where in (
        (tc, NC, c, lambda i: device(c=i)),
        (tx, NX, x, lambda i: device(x=i)),
        (ty, NY, y, lambda i: device(y=i)),
        (tz, NZ, z, lambda i: device(z=i)),
    ):
        if slots is not tc:
            slots[me] = total
        copies = []
        for d in range(1, n):
            copies.append(links.send(slots.at[me], slots.at[me], where(lax.rem(me + d, n))))
        for copy in copies:
            copy.wait_recv()
        total = slots[0]
        for i in range(1, n):
            total = total + slots[i]
    tile_o[...] = total
    clip = clip_of(total)

    W96[...] = jnp.zeros_like(W96)
    for p in range(2):
        for h in range(2):
            q = 2 * p + h
            col = slice(h * LANES, (h + 1) * LANES)
            g = S72[R * q : R * q + R, :]
            psum_o[p, :, col] = g
            W96[R * q : R * q + R, :] = adamw_step(
                p_master[p, :, col], p_m[p, :, col], p_v[p, :, col], clip * g, decay_rate
            )[0]
    g = K3[z, 0:R, :]
    ksum_o[...] = g
    W96[72 : 72 + R, :] = adamw_step(k_master[...], k_m[...], k_v[...], clip * g, decay_rate)[0]
    G[c, z, y] = W96[...].astype(BF16)

    up_y, down_y = device(y=lax.rem(y + 1, NY)), device(y=lax.rem(y + NY - 1, NY))
    ahead, behind = lax.rem(y + 1, NY), lax.rem(y + NY - 1, NY)
    own = G.at[c, z, y]
    first = [links.send(own, own, up_y), links.send(own, own, down_y)]
    first[0].wait_recv()
    lo = G.at[c, z, behind, 0:48]
    second = [links.send(lo, lo, up_y)]
    first[1].wait_recv()
    hi = G.at[c, z, ahead, 48:96]
    second.append(links.send(hi, hi, down_y))

    up_z, down_z = device(z=lax.rem(z + 1, NZ)), device(z=lax.rem(z + NZ - 1, NZ))
    far = lax.rem(y + 2, NY)
    order = (y, behind, ahead, far)

    def plane_moves(zz, yy, dev):
        ref = G.at[c, zz, yy]
        return links.send(ref, ref, dev)

    up, down, twin = {}, {}, {}
    for j in range(3):
        up[1, j] = plane_moves(z, order[j], up_z)
        down[1, j] = plane_moves(z, order[j], down_z)
    second[0].wait_recv()
    second[1].wait_recv()
    up[1, 3] = plane_moves(z, order[3], up_z)
    down[1, 3] = plane_moves(z, order[3], down_z)
    own_plane = G.at[c, z]
    twin[0, 0] = links.send(own_plane, own_plane, sibling)

    def unpack(zz):
        for k in range(NY * NC):
            block = G[k % NC, zz, k // NC].astype(F32)
            W96[...] = block
            for q in range(5):
                T5[q, R * k : R * k + R, :] = W96[R * q : R * q + R, :]
        for p in range(2):
            for h in range(2):
                pw_o[p, zz, :, h * LANES : (h + 1) * LANES] = T5[2 * p + h].astype(BF16)
        FK[x, zz] = T5[4].astype(BF16)

    up_x, down_x = device(x=lax.rem(x + 1, NX)), device(x=lax.rem(x + NX - 1, NX))
    cut_x = (slice(0, 80), slice(80, 144))
    x_first = {}

    def x_block(j):
        return lax.rem(z + (1 - 2 * c) * j - c + NZ, NZ)

    def x_start(j):
        ref = FK.at[x, x_block(j)]
        x_first[j] = (links.send(ref, ref, up_x), links.send(ref, ref, down_x))

    for d in range(1, 5):
        below, above = lax.rem(z - d + NZ, NZ), lax.rem(z + d, NZ)
        if d < 4:
            for j in range(4):
                up[d, j].wait_recv()
                if d < 3:
                    up[d + 1, j] = plane_moves(below, order[j], up_z)
                elif j < 2:
                    up[4, j] = plane_moves(below, order[j], up_z)
                down[d, j].wait_recv()
                if d < 3:
                    down[d + 1, j] = plane_moves(above, order[j], down_z)
                elif j >= 2:
                    down[4, j] = plane_moves(above, order[j], down_z)
            for way, zz in ((0, below), (1, above)):
                ref = G.at[c, zz]
                twin[d, way] = links.send(ref, ref, sibling)
        else:
            for copy in (up[4, 0], up[4, 1], down[4, 2], down[4, 3]):
                copy.wait_recv()
            ref = G.at[c, above]
            twin[4, 0] = links.send(ref, ref, sibling)
        if d == 1:
            twin[0, 0].wait_recv()
            unpack(z)
        else:
            for way, zz in ((0, lax.rem(z - d + 1 + NZ, NZ)), (1, lax.rem(z + d - 1, NZ))):
                twin[d - 1, way].wait_recv()
                unpack(zz)
            x_start(d - 2)
    twin[4, 0].wait_recv()
    unpack(lax.rem(z + 4, NZ))
    x_start(3)

    x_behind, x_ahead, x_far = lax.rem(x + NX - 1, NX), lax.rem(x + 1, NX), lax.rem(x + 2, NX)
    x_second, x_twin = {}, []
    for j in range(4):
        zz = x_block(j)
        x_first[j][0].wait_recv()
        ref = FK.at[x_behind, zz, cut_x[0]]
        lo_send = links.send(ref, ref, up_x)
        ref = FK.at[x_behind, zz]
        x_twin.append(links.send(ref, ref, sibling))
        x_first[j][1].wait_recv()
        ref = FK.at[x_ahead, zz, cut_x[1]]
        hi_send = links.send(ref, ref, down_x)
        ref = FK.at[x_ahead, zz]
        x_twin.append(links.send(ref, ref, sibling))
        x_second[j] = (lo_send, hi_send)
    for j in range(4):
        zz = x_block(j)
        for copy in x_second[j]:
            copy.wait_recv()
        ref = FK.at[x_far, zz]
        x_twin.append(links.send(ref, ref, sibling))
    for copy in x_twin:
        copy.wait_recv()

    @pl.loop(0, NZ)
    def _(zz):
        for xx in range(NX):
            kw_o[zz, :, xx * LANES : (xx + 1) * LANES] = FK[xx, zz]

    assert len(links.started) <= N_COPIES
    links.finish()


def moments_kernel(
    psum, ksum, tile, p_master, p_m, p_v, k_master, k_m, k_v, gains, g_m, g_v,
    p_new, p_m_new, p_v_new, k_new, k_m_new, k_v_new, gains_new, g_m_new, g_v_new,
):
    clip = clip_of(tile[...])
    for p in range(2):
        p_new[p], p_m_new[p], p_v_new[p] = adamw_step(p_master[p], p_m[p], p_v[p], clip * psum[p], decay_rate)
    k_new[...], k_m_new[...], k_v_new[...] = adamw_step(k_master[...], k_m[...], k_v[...], clip * ksum[...], decay_rate)
    for i in range(2):
        for h in range(2):
            col = slice(h * LANES, (h + 1) * LANES)
            row = slice(i, i + 1)
            g = tile[2 * i + h : 2 * i + h + 1, :]
            gains_new[row, col], g_m_new[row, col], g_v_new[row, col] = adamw_step(
                gains[row, col], g_m[row, col], g_v[row, col], clip * g, 0.0
            )


def shards(
    proj_grads,
    kv_grads,
    gain_grads,
    proj_master,
    proj_m,
    proj_v,
    kv_master,
    kv_m,
    kv_v,
    gains,
    gains_m,
    gains_v,
):
    vmem, anywhere = pl.BlockSpec(memory_space=pltpu.VMEM), pl.BlockSpec(memory_space=pl.ANY)
    shape = jax.ShapeDtypeStruct
    scratch = [
        ((2, 2, 1152, 256), BF16), ((2, 1152, 512), BF16),
        ((NC, NY, NZ, 40, LANES), F32), ((NC, NZ, NY, 32, LANES), F32), ((NC, NX, NY, 2, 72, LANES), F32),
        ((NY, NZ, 40, LANES), F32), ((NZ, NY, 32, LANES), F32), ((NX, NY, 2, 72, LANES), F32),
        ((ZR, LANES), F32),
        ((2, 2, 2, 4, 40, LANES), F32), ((2, 2, 4, 2, 32, LANES), F32), ((2, 2, 2, 2, 2, 72, LANES), F32),
        ((2, 4, 24, LANES), F32), ((2, 4, 16, LANES), F32), ((2, 2, 2, 16, LANES), F32), ((2, 2, 2, 72, LANES), F32),
        ((NZ, 24, LANES), F32), ((2, 4, 16, LANES), F32), ((2, 4, 8, LANES), F32),
        ((NC, 8, LANES), F32), ((NX, 8, LANES), F32), ((NY, 8, LANES), F32), ((NZ, 8, LANES), F32),
        ((72, LANES), F32), ((96, LANES), F32),
        ((NC, NZ, NY, 96, LANES), BF16), ((NX, NZ, ZR, LANES), BF16), ((5, ZR, LANES), F32),
    ]
    psum, ksum, tile, proj_weights, kv_weights = pl.pallas_call(
        step_kernel,
        name="reduce_update_gather",
        out_shape=[
            shape((2, R, 256), F32),
            shape((R, LANES), F32),
            shape((8, LANES), F32),
            shape((2, NZ, ZR, 256), BF16),
            shape((NZ, ZR, 512), BF16),
        ],
        in_specs=[anywhere, anywhere] + [vmem] * 7,
        out_specs=[vmem] * 5,
        scratch_shapes=[pltpu.VMEM(s, d) for s, d in scratch]
        + [pltpu.SemaphoreType.DMA((N_COPIES,)), pltpu.SemaphoreType.DMA((N_COPIES,)), pltpu.SemaphoreType.DMA((2,))],
        compiler_params=pltpu.CompilerParams(
            collective_id=0, has_side_effects=True, vmem_limit_bytes=56 * 1024 * 1024
        ),
    )(proj_grads, kv_grads, gain_grads, proj_master, proj_m, proj_v, kv_master, kv_m, kv_v)
    state = (proj_master, proj_m, proj_v, kv_master, kv_m, kv_v, gains, gains_m, gains_v)
    new = pl.pallas_call(
        moments_kernel,
        name="moments",
        out_shape=[shape(a.shape, F32) for a in state],
        in_specs=[vmem] * 12,
        out_specs=[vmem] * 9,
    )(psum, ksum, tile, *state)
    return (
        *new[0:3],
        proj_weights.reshape(2, 1152, 256),
        *new[3:6],
        kv_weights.reshape(1152, 512),
        *new[6:9],
    )


def solution(mesh):
    placed = (
        P("shard", None, None, "tensor"),
        P(("tensor", "shard"), None, None),
        P(("tensor", "shard"), None, None),
        P(None, "shard", "tensor"),
        P(None, "shard", "tensor"),
        P(None, "shard", "tensor"),
        P("shard", "tensor"),
        P("shard", "tensor"),
        P("shard", "tensor"),
        P(),
        P(),
        P(),
    )
    return jax.shard_map(
        shards,
        mesh=mesh,
        in_specs=placed,
        out_specs=(
            P(None, "shard", "tensor"),
            P(None, "shard", "tensor"),
            P(None, "shard", "tensor"),
            P(None, None, "tensor"),
            P("shard", "tensor"),
            P("shard", "tensor"),
            P("shard", "tensor"),
            P(),
            P(),
            P(),
            P(),
        ),
        check_vma=False,
    )
```

```python
import math

import jax
import jax.numpy as jnp
from jax import lax
from jax.experimental import pallas as pl
from jax.experimental.pallas import tpu as pltpu
from jax.sharding import PartitionSpec as P

PARAMS = 2949632
MESH = pl.DeviceIdType.MESH
F32, BF16 = jnp.float32, jnp.bfloat16

NZ, NY, NC, NX = 8, 4, 2, 4
R = 18
ZR = NY * NC * R
LANES = 128

beta_one = 0.9
beta_two = 0.95
learn_rate = 0.01
decay_rate = 0.1
epsilon = 1e-08
step_count = 10


def adamw_step(master, moment, second, update_grad, decay):
    moment_new = beta_one * moment + (1.0 - beta_one) * update_grad
    second_new = beta_two * second + (1.0 - beta_two) * update_grad * update_grad
    first_hat = moment_new / (1.0 - beta_one**step_count)
    second_hat = second_new / (1.0 - beta_two**step_count)
    master_new = master - learn_rate * (
        first_hat / (jnp.sqrt(second_hat) + epsilon) + decay * master
    )
    return (master_new, moment_new, second_new)


def clip_of(tile):
    row = lax.broadcasted_iota(jnp.int32, tile.shape, 0)
    terms = jnp.where(row < 4, tile * tile, jnp.where(row == 4, tile, 0.0))
    norm_square = jnp.sum(jnp.sum(terms, axis=0, keepdims=True), axis=1, keepdims=True)
    return jnp.minimum(1.0, math.sqrt(PARAMS) / jnp.sqrt(norm_square))


class Links:
    def __init__(self, send_sems, recv_sems, local_sems):
        self.send_sems, self.recv_sems, self.local_sems = send_sems, recv_sems, local_sems
        self.started, self.locals = [], 0

    def send(self, src, dst, device):
        number = len(self.started)
        copy = pltpu.make_async_remote_copy(
            src_ref=src,
            dst_ref=dst,
            send_sem=self.send_sems.at[number],
            recv_sem=self.recv_sems.at[number],
            device_id=device,
            device_id_type=MESH,
        )
        copy.start()
        self.started.append(copy)
        return copy

    def local(self, src, dst):
        copy = pltpu.make_async_copy(src, dst, self.local_sems.at[self.locals])
        self.locals += 1
        copy.start()
        return copy

    def finish(self):
        for copy in self.started:
            copy.wait_send()


N_COPIES = 176


def scatter_ring(links, n, pos, device, view, slot):
    half = n // 2
    copies = {}

    def step(way, part, d):
        dest = lax.rem(pos + way * d + n, n)
        copies[way, part, d] = links.send(view(dest, part), slot(way, part, d), device(lax.rem(pos + way + n, n)))

    def take(way, part, d):
        copies[way, part, d].wait_recv()
        dest = lax.rem(pos + way * (d - 1) + n, n)
        ref, got = view(dest, part), slot(way, part, d)
        ref[...] = ref[...] + got[...]

    for way in (1, -1):
        step(way, 0 if way == 1 else 1, half)
    if half > 1:
        for way in (1, -1):
            step(way, 1 if way == 1 else 0, half - 1)
    for d in range(half - 1, 0, -1):
        yield
        for way in (1, -1):
            lead = 0 if way == 1 else 1
            take(way, lead, d + 1)
            step(way, lead, d)
        if d < half - 1:
            for way in (1, -1):
                other = 1 if way == 1 else 0
                take(way, other, d + 1)
                step(way, other, d)
    yield
    for way in (1, -1):
        for part in (0, 1):
            if (way, part, 1) in copies:
                take(way, part, 1)


def scatter_direct(links, n, pos, device, view, slots):
    copies = {}
    for d in sorted(range(1, n), key=lambda d: -min(d, n - d)):
        dest = lax.rem(pos + d, n)
        copies[d] = links.send(view(dest), slots.at[d - 1], device(dest))
    yield
    own = view(pos)
    total = own[...]
    for d in sorted(range(1, n), key=lambda d: min(d, n - d)):
        copies[d].wait_recv()
        total = total + slots[d - 1]
    own[...] = total


def step_kernel(
    pg, kg, gg, p_master, p_m, p_v, k_master, k_m, k_v,
    psum_o, ksum_o, tile_o, pw_o, kw_o,
    pgv, kgv, PA, PB, KK, RA, RB, RK, T,
    rAy, rBz, rKx, rAz, rBy, rKy, K3, rKz,
    tc, tx, ty, tz, S72, W96, G, FK, T5,
    send_sems, recv_sems, local_sems,
):
    shard, x = lax.axis_index("shard"), lax.axis_index("tensor")
    c = lax.rem(shard, NC)
    y = lax.rem(shard // NC, NY)
    z = shard // (NC * NY)
    oc = 1 - c

    def device(z=z, y=y, c=c, x=x):
        return {"shard": (z * NY + y) * NC + c, "tensor": x}

    links = Links(send_sems, recv_sems, local_sems)
    sibling = device(c=oc)
    others = [sibling]
    others += [device(x=lax.rem(x + d, NX)) for d in range(1, NX)]
    others += [device(y=lax.rem(y + d, NY)) for d in range(1, NY)]
    others += [device(z=lax.rem(z + d, NZ)) for d in range(1, NZ)]

    k_in = links.local(kg, kgv)
    p_in = links.local(pg, pgv)
    barrier = pltpu.get_barrier_semaphore()
    for other in others:
        pl.semaphore_signal(barrier, inc=1, device_id=other, device_id_type=MESH)

    gain = gg[0].astype(F32) + gg[1].astype(F32)
    tc[c] = jnp.zeros((8, LANES), F32)
    for i in range(2):
        for h in range(2):
            tc[c, 2 * i + h : 2 * i + h + 1, :] = gain[i : i + 1, h * LANES : (h + 1) * LANES]

    k_in.wait()
    barrier_done = False
    k_cores = []
    for dx in (2, 1, 3, 0):
        xx = lax.rem(x + dx, NX)
        col = pl.ds(pl.multiple_of(xx * LANES, LANES), LANES)

        @pl.loop(0, 2)
        def _(zh):
            for zl in range(4):
                rows = pl.ds(pl.multiple_of((zh * 4 + zl) * ZR, 16), ZR)
                T[...] = kgv[0, rows, col].astype(F32) + kgv[1, rows, col].astype(F32)
                for k in range(NY * NC):
                    KK[k % NC, xx, k // NC, zh, R * zl : R * zl + R, :] = T[R * k : R * k + R, :]

        if not barrier_done:
            pl.semaphore_wait(barrier, len(others))
            barrier_done = True
        k_cores.append((xx, links.send(KK.at[oc, xx], RK.at[xx], sibling)))

    p_in.wait()
    for p in range(2):

        @pl.loop(0, NZ)
        def _(zz):
            rows = pl.ds(pl.multiple_of(zz * ZR, 16), ZR)
            for h in range(2):
                col = slice(h * LANES, (h + 1) * LANES)
                T[...] = pgv[0, p, rows, col].astype(F32) + pgv[1, p, rows, col].astype(F32)
                for k in range(NY * NC):
                    yy, cc = k // NC, k % NC
                    q = 2 * p + h
                    if q < 2:
                        PA[cc, yy, zz, R * q : R * q + R, :] = T[R * k : R * k + R, :]
                    elif q == 2:
                        PA[cc, yy, zz, 36:40, :] = T[R * k : R * k + 4, :]
                        PB[cc, zz, yy, 0:14, :] = T[R * k + 4 : R * k + R, :]
                    else:
                        PB[cc, zz, yy, 14:32, :] = T[R * k : R * k + R, :]

    b_core = links.send(PB.at[oc], RB, sibling)
    a_core = links.send(PA.at[oc], RA, sibling)

    for xx, copy in k_cores:
        copy.wait_recv()
        KK[c, xx] = KK[c, xx] + RK[xx]

    def chain_k():
        yield from scatter_ring(
            links, NX, x, lambda i: device(x=i),
            lambda i, part: KK.at[c, i, 2 * part : 2 * part + 2],
            lambda way, part, d: rKx.at[(1 - way) // 2, part, d - 1],
        )
        yield from scatter_direct(links, NY, y, lambda i: device(y=i), lambda i: KK.at[c, x, i], rKy)
        K3[...] = jnp.zeros_like(K3)
        for zz in range(NZ):
            K3[zz, 0:R, :] = KK[c, x, y, zz // 4, R * (zz % 4) : R * (zz % 4) + R, :]
        yield from scatter_direct(links, NZ, z, lambda i: device(z=i), lambda i: K3.at[i], rKz)

    def chain_b():
        yield from scatter_ring(
            links, NZ, z, lambda i: device(z=i),
            lambda i, part: PB.at[c, i, 2 * part : 2 * part + 2],
            lambda way, part, d: rBz.at[(1 - way) // 2, part, d - 1],
        )
        yield from scatter_direct(links, NY, y, lambda i: device(y=i), lambda i: PB.at[c, z, i], rBy)

    def chain_a():
        yield from scatter_ring(
            links, NY, y, lambda i: device(y=i),
            lambda i, part: PA.at[c, i, 4 * part : 4 * part + 4],
            lambda way, part, d: rAy.at[(1 - way) // 2, part, d - 1],
        )
        yield from scatter_direct(links, NZ, z, lambda i: device(z=i), lambda i: PA.at[c, y, i], rAz)

    for_k, for_b, for_a = chain_k(), chain_b(), chain_a()
    next(for_k)
    b_core.wait_recv()

    @pl.loop(0, NZ)
    def _(zz):
        PB[c, zz] = PB[c, zz] + RB[zz]

    next(for_b)
    a_core.wait_recv()

    @pl.loop(0, NY)
    def _(yy):
        PA[c, yy] = PA[c, yy] + RA[yy]

    next(for_a)
    for chain in (for_b, for_b, for_a, for_k, for_b, for_b, for_a, for_k, for_b, for_a, for_k, for_k):
        next(chain, None)

    S72[0:40, :] = PA[c, y, z]
    S72[40:72, :] = PB[c, z, y]
    p_sum, k_sum = S72[...], K3[z]
    squares = jnp.sum(p_sum * p_sum, axis=0, keepdims=True) + jnp.sum(k_sum * k_sum, axis=0, keepdims=True)
    tc[c, 4:5, :] = squares
    for slots, n, me, where in (
        (tc, NC, c, lambda i: device(c=i)),
        (tx, NX, x, lambda i: device(x=i)),
        (ty, NY, y, lambda i: device(y=i)),
        (tz, NZ, z, lambda i: device(z=i)),
    ):
        if slots is not tc:
            slots[me] = total
        copies = []
        for d in range(1, n):
            copies.append(links.send(slots.at[me], slots.at[me], where(lax.rem(me + d, n))))
        for copy in copies:
            copy.wait_recv()
        total = slots[0]
        for i in range(1, n):
            total = total + slots[i]
    tile_o[...] = total
    clip = clip_of(total)

    W96[...] = jnp.zeros_like(W96)
    for p in range(2):
        for h in range(2):
            q = 2 * p + h
            col = slice(h * LANES, (h + 1) * LANES)
            g = S72[R * q : R * q + R, :]
            psum_o[:, p, col] = g
            W96[R * q : R * q + R, :] = adamw_step(
                p_master[:, p, col], p_m[:, p, col], p_v[:, p, col], clip * g, decay_rate
            )[0]
    g = K3[z, 0:R, :]
    ksum_o[...] = g
    W96[72 : 72 + R, :] = adamw_step(k_master[...], k_m[...], k_v[...], clip * g, decay_rate)[0]
    G[c, z, y] = W96[...].astype(BF16)

    up_y, down_y = device(y=lax.rem(y + 1, NY)), device(y=lax.rem(y + NY - 1, NY))
    ahead, behind = lax.rem(y + 1, NY), lax.rem(y + NY - 1, NY)
    own = G.at[c, z, y]
    first = [links.send(own, own, up_y), links.send(own, own, down_y)]
    first[0].wait_recv()
    lo = G.at[c, z, behind, 0:48]
    second = [links.send(lo, lo, up_y)]
    first[1].wait_recv()
    hi = G.at[c, z, ahead, 48:96]
    second.append(links.send(hi, hi, down_y))

    up_z, down_z = device(z=lax.rem(z + 1, NZ)), device(z=lax.rem(z + NZ - 1, NZ))
    far = lax.rem(y + 2, NY)
    order = (y, behind, ahead, far)

    def plane_moves(zz, yy, dev):
        ref = G.at[c, zz, yy]
        return links.send(ref, ref, dev)

    up, down, twin = {}, {}, {}
    for j in range(3):
        up[1, j] = plane_moves(z, order[j], up_z)
        down[1, j] = plane_moves(z, order[j], down_z)
    second[0].wait_recv()
    second[1].wait_recv()
    up[1, 3] = plane_moves(z, order[3], up_z)
    down[1, 3] = plane_moves(z, order[3], down_z)
    own_plane = G.at[c, z]
    twin[0, 0] = links.send(own_plane, own_plane, sibling)

    def unpack(zz):
        for k in range(NY * NC):
            block = G[k % NC, zz, k // NC].astype(F32)
            W96[...] = block
            for q in range(5):
                T5[q, R * k : R * k + R, :] = W96[R * q : R * q + R, :]
        for p in range(2):
            for h in range(2):
                pw_o[p, zz, :, h * LANES : (h + 1) * LANES] = T5[2 * p + h].astype(BF16)
        FK[x, zz] = T5[4].astype(BF16)

    up_x, down_x = device(x=lax.rem(x + 1, NX)), device(x=lax.rem(x + NX - 1, NX))
    cut_x = (slice(0, 80), slice(80, 144))
    x_first = {}

    def x_block(j):
        return lax.rem(z + (1 - 2 * c) * j - c + NZ, NZ)

    def x_start(j):
        ref = FK.at[x, x_block(j)]
        x_first[j] = (links.send(ref, ref, up_x), links.send(ref, ref, down_x))

    for d in range(1, 5):
        below, above = lax.rem(z - d + NZ, NZ), lax.rem(z + d, NZ)
        if d < 4:
            for j in range(4):
                up[d, j].wait_recv()
                if d < 3:
                    up[d + 1, j] = plane_moves(below, order[j], up_z)
                elif j < 2:
                    up[4, j] = plane_moves(below, order[j], up_z)
                down[d, j].wait_recv()
                if d < 3:
                    down[d + 1, j] = plane_moves(above, order[j], down_z)
                elif j >= 2:
                    down[4, j] = plane_moves(above, order[j], down_z)
            for way, zz in ((0, below), (1, above)):
                ref = G.at[c, zz]
                twin[d, way] = links.send(ref, ref, sibling)
        else:
            for copy in (up[4, 0], up[4, 1], down[4, 2], down[4, 3]):
                copy.wait_recv()
            ref = G.at[c, above]
            twin[4, 0] = links.send(ref, ref, sibling)
        if d == 1:
            twin[0, 0].wait_recv()
            unpack(z)
        else:
            for way, zz in ((0, lax.rem(z - d + 1 + NZ, NZ)), (1, lax.rem(z + d - 1, NZ))):
                twin[d - 1, way].wait_recv()
                unpack(zz)
            x_start(d - 2)
    twin[4, 0].wait_recv()
    unpack(lax.rem(z + 4, NZ))
    x_start(3)

    x_behind, x_ahead, x_far = lax.rem(x + NX - 1, NX), lax.rem(x + 1, NX), lax.rem(x + 2, NX)
    x_second, x_twin = {}, []
    for j in range(4):
        zz = x_block(j)
        x_first[j][0].wait_recv()
        ref = FK.at[x_behind, zz, cut_x[0]]
        lo_send = links.send(ref, ref, up_x)
        ref = FK.at[x_behind, zz]
        x_twin.append(links.send(ref, ref, sibling))
        x_first[j][1].wait_recv()
        ref = FK.at[x_ahead, zz, cut_x[1]]
        hi_send = links.send(ref, ref, down_x)
        ref = FK.at[x_ahead, zz]
        x_twin.append(links.send(ref, ref, sibling))
        x_second[j] = (lo_send, hi_send)
    for j in range(4):
        zz = x_block(j)
        for copy in x_second[j]:
            copy.wait_recv()
        ref = FK.at[x_far, zz]
        x_twin.append(links.send(ref, ref, sibling))
    for copy in x_twin:
        copy.wait_recv()

    @pl.loop(0, NZ)
    def _(zz):
        for xx in range(NX):
            kw_o[zz, :, xx * LANES : (xx + 1) * LANES] = FK[xx, zz]

    assert len(links.started) <= N_COPIES
    links.finish()


def moments_kernel(
    psum, ksum, tile, pw, kw, p_master, p_m, p_v, k_master, k_m, k_v, gains, g_m, g_v,
    p_new, p_m_new, p_v_new, k_new, k_m_new, k_v_new, gains_new, g_m_new, g_v_new, pw_new, kw_new,
    pwv, kwv, in_sems, out_sems,
):
    pieces = []
    for i in range(4):
        p, half = i // 2, pl.ds(4 * (i % 2), 4)
        pieces.append((pw.at[p, half], pwv.at[p, half], pw_new.at[p, half]))
        pair = pl.ds(2 * i, 2)
        pieces.append((kw.at[pair], kwv.at[pair], kw_new.at[pair]))
    into = [pltpu.make_async_copy(src, mid, in_sems.at[i]) for i, (src, mid, _) in enumerate(pieces)]
    out = [pltpu.make_async_copy(mid, dst, out_sems.at[i]) for i, (_, mid, dst) in enumerate(pieces)]
    for copy in into:
        copy.start()
    for arrive, leave in zip(into, out):
        arrive.wait()
        leave.start()
    clip = clip_of(tile[...])
    scale = jnp.reshape(clip, (1, 1, 1))
    p_new[...], p_m_new[...], p_v_new[...] = adamw_step(
        p_master[...], p_m[...], p_v[...], scale * psum[...], decay_rate
    )
    k_new[...], k_m_new[...], k_v_new[...] = adamw_step(k_master[...], k_m[...], k_v[...], clip * ksum[...], decay_rate)
    for i in range(2):
        for h in range(2):
            col = slice(h * LANES, (h + 1) * LANES)
            row = slice(i, i + 1)
            g = tile[2 * i + h : 2 * i + h + 1, :]
            gains_new[row, col], g_m_new[row, col], g_v_new[row, col] = adamw_step(
                gains[row, col], g_m[row, col], g_v[row, col], clip * g, 0.0
            )
    for leave in out:
        leave.wait()


def shards(
    proj_grads,
    kv_grads,
    gain_grads,
    proj_master,
    proj_m,
    proj_v,
    kv_master,
    kv_m,
    kv_v,
    gains,
    gains_m,
    gains_v,
):
    proj_master, proj_m, proj_v = (jnp.transpose(a, (1, 0, 2)) for a in (proj_master, proj_m, proj_v))
    vmem, anywhere = pl.BlockSpec(memory_space=pltpu.VMEM), pl.BlockSpec(memory_space=pl.ANY)
    shape = jax.ShapeDtypeStruct
    scratch = [
        ((2, 2, 1152, 256), BF16), ((2, 1152, 512), BF16),
        ((NC, NY, NZ, 40, LANES), F32), ((NC, NZ, NY, 32, LANES), F32), ((NC, NX, NY, 2, 72, LANES), F32),
        ((NY, NZ, 40, LANES), F32), ((NZ, NY, 32, LANES), F32), ((NX, NY, 2, 72, LANES), F32),
        ((ZR, LANES), F32),
        ((2, 2, 2, 4, 40, LANES), F32), ((2, 2, 4, 2, 32, LANES), F32), ((2, 2, 2, 2, 2, 72, LANES), F32),
        ((NZ - 1, 40, LANES), F32), ((NY - 1, 32, LANES), F32), ((NY - 1, 2, 72, LANES), F32),
        ((NZ, 24, LANES), F32), ((NZ - 1, 24, LANES), F32),
        ((NC, 8, LANES), F32), ((NX, 8, LANES), F32), ((NY, 8, LANES), F32), ((NZ, 8, LANES), F32),
        ((72, LANES), F32), ((96, LANES), F32),
        ((NC, NZ, NY, 96, LANES), BF16), ((NX, NZ, ZR, LANES), BF16), ((5, ZR, LANES), F32),
    ]
    psum, ksum, tile, proj_weights, kv_weights = pl.pallas_call(
        step_kernel,
        name="reduce_update_gather",
        out_shape=[
            shape((R, 2, 256), F32),
            shape((R, LANES), F32),
            shape((8, LANES), F32),
            shape((2, NZ, ZR, 256), BF16),
            shape((NZ, ZR, 512), BF16),
        ],
        in_specs=[anywhere, anywhere] + [vmem] * 7,
        out_specs=[vmem] * 5,
        scratch_shapes=[pltpu.VMEM(s, d) for s, d in scratch]
        + [pltpu.SemaphoreType.DMA((N_COPIES,)), pltpu.SemaphoreType.DMA((N_COPIES,)), pltpu.SemaphoreType.DMA((2,))],
        compiler_params=pltpu.CompilerParams(
            collective_id=0, has_side_effects=True, vmem_limit_bytes=56 * 1024 * 1024
        ),
    )(proj_grads, kv_grads, gain_grads, proj_master, proj_m, proj_v, kv_master, kv_m, kv_v)
    state = (proj_master, proj_m, proj_v, kv_master, kv_m, kv_v, gains, gains_m, gains_v)
    new = pl.pallas_call(
        moments_kernel,
        name="moments",
        out_shape=[shape(a.shape, F32) for a in state] + [shape(a.shape, BF16) for a in (proj_weights, kv_weights)],
        in_specs=[vmem] * 3 + [anywhere] * 2 + [vmem] * 9,
        out_specs=[vmem] * 9 + [anywhere] * 2,
        scratch_shapes=[
            pltpu.VMEM(proj_weights.shape, BF16),
            pltpu.VMEM(kv_weights.shape, BF16),
            pltpu.SemaphoreType.DMA((8,)),
            pltpu.SemaphoreType.DMA((8,)),
        ],
    )(psum, ksum, tile, proj_weights, kv_weights, *state)
    return (
        *(jnp.transpose(a, (1, 0, 2)) for a in new[0:3]),
        new[9].reshape(2, 1152, 256),
        *new[3:6],
        new[10].reshape(1152, 512),
        *new[6:9],
    )


def solution(mesh):
    placed = (
        P("shard", None, None, "tensor"),
        P(("tensor", "shard"), None, None),
        P(("tensor", "shard"), None, None),
        P(None, "shard", "tensor"),
        P(None, "shard", "tensor"),
        P(None, "shard", "tensor"),
        P("shard", "tensor"),
        P("shard", "tensor"),
        P("shard", "tensor"),
        P(),
        P(),
        P(),
    )
    return jax.shard_map(
        shards,
        mesh=mesh,
        in_specs=placed,
        out_specs=(
            P(None, "shard", "tensor"),
            P(None, "shard", "tensor"),
            P(None, "shard", "tensor"),
            P(None, None, "tensor"),
            P("shard", "tensor"),
            P("shard", "tensor"),
            P("shard", "tensor"),
            P(),
            P(),
            P(),
            P(),
        ),
        check_vma=False,
    )
```

```python
import math

import jax
import jax.numpy as jnp
from jax import lax
from jax.experimental import pallas as pl
from jax.experimental.pallas import tpu as pltpu
from jax.sharding import PartitionSpec as P

PARAMS = 2949632
MESH = pl.DeviceIdType.MESH
F32, BF16 = jnp.float32, jnp.bfloat16

NZ, NY, NC, NX = 8, 4, 2, 4
R = 18
ZR = NY * NC * R
LANES = 128

beta_one = 0.9
beta_two = 0.95
learn_rate = 0.01
decay_rate = 0.1
epsilon = 1e-08
step_count = 10


def adamw_step(master, moment, second, update_grad, decay):
    moment_new = beta_one * moment + (1.0 - beta_one) * update_grad
    second_new = beta_two * second + (1.0 - beta_two) * update_grad * update_grad
    first_hat = moment_new / (1.0 - beta_one**step_count)
    second_hat = second_new / (1.0 - beta_two**step_count)
    master_new = master - learn_rate * (
        first_hat / (jnp.sqrt(second_hat) + epsilon) + decay * master
    )
    return (master_new, moment_new, second_new)


def clip_of(tile):
    row = lax.broadcasted_iota(jnp.int32, tile.shape, 0)
    terms = jnp.where(row < 4, tile * tile, jnp.where(row == 4, tile, 0.0))
    norm_square = jnp.sum(jnp.sum(terms, axis=0, keepdims=True), axis=1, keepdims=True)
    return jnp.minimum(1.0, math.sqrt(PARAMS) / jnp.sqrt(norm_square))


class Links:
    def __init__(self, send_sems, recv_sems, local_sems):
        self.send_sems, self.recv_sems, self.local_sems = send_sems, recv_sems, local_sems
        self.started, self.locals = [], 0

    def send(self, src, dst, device):
        number = len(self.started)
        copy = pltpu.make_async_remote_copy(
            src_ref=src,
            dst_ref=dst,
            send_sem=self.send_sems.at[number],
            recv_sem=self.recv_sems.at[number],
            device_id=device,
            device_id_type=MESH,
        )
        copy.start()
        self.started.append(copy)
        return copy

    def local(self, src, dst):
        copy = pltpu.make_async_copy(src, dst, self.local_sems.at[self.locals])
        self.locals += 1
        copy.start()
        return copy

    def finish(self):
        for copy in self.started:
            copy.wait_send()


N_COPIES = 176


def scatter_ring(links, n, pos, device, view, slot):
    half = n // 2
    copies = {}

    def step(way, part, d):
        dest = lax.rem(pos + way * d + n, n)
        copies[way, part, d] = links.send(view(dest, part), slot(way, part, d), device(lax.rem(pos + way + n, n)))

    def take(way, part, d):
        copies[way, part, d].wait_recv()
        dest = lax.rem(pos + way * (d - 1) + n, n)
        ref, got = view(dest, part), slot(way, part, d)
        ref[...] = ref[...] + got[...]

    for way in (1, -1):
        step(way, 0 if way == 1 else 1, half)
    if half > 1:
        for way in (1, -1):
            step(way, 1 if way == 1 else 0, half - 1)
    for d in range(half - 1, 0, -1):
        yield
        for way in (1, -1):
            lead = 0 if way == 1 else 1
            take(way, lead, d + 1)
            step(way, lead, d)
        if d < half - 1:
            for way in (1, -1):
                other = 1 if way == 1 else 0
                take(way, other, d + 1)
                step(way, other, d)
    yield
    for way in (1, -1):
        for part in (0, 1):
            if (way, part, 1) in copies:
                take(way, part, 1)


def scatter_direct(links, n, pos, device, view, slots):
    copies = {}
    for d in sorted(range(1, n), key=lambda d: -min(d, n - d)):
        dest = lax.rem(pos + d, n)
        copies[d] = links.send(view(dest), slots.at[d - 1], device(dest))
    yield
    own = view(pos)
    total = own[...]
    for d in sorted(range(1, n), key=lambda d: min(d, n - d)):
        copies[d].wait_recv()
        total = total + slots[d - 1]
    own[...] = total


def step_kernel(
    pg, kg, gg, p_master, p_m, p_v, k_master, k_m, k_v,
    psum_o, ksum_o, tile_o, pw_o, kw_o,
    pgv, kgv, PA, PB, KK, RA, RB, RK, T,
    rAy, rBz, rKx, rAz, rBy, rKy, K3, rKz,
    tc, tx, ty, tz, S72, W96, G, FK, T5,
    send_sems, recv_sems, local_sems,
):
    shard, x = lax.axis_index("shard"), lax.axis_index("tensor")
    c = lax.rem(shard, NC)
    y = lax.rem(shard // NC, NY)
    z = shard // (NC * NY)
    oc = 1 - c

    def device(z=z, y=y, c=c, x=x):
        return {"shard": (z * NY + y) * NC + c, "tensor": x}

    links = Links(send_sems, recv_sems, local_sems)
    sibling = device(c=oc)
    others = [sibling]
    others += [device(x=lax.rem(x + d, NX)) for d in range(1, NX)]
    others += [device(y=lax.rem(y + d, NY)) for d in range(1, NY)]
    others += [device(z=lax.rem(z + d, NZ)) for d in range(1, NZ)]

    k_in = links.local(kg, kgv)
    p_in = links.local(pg, pgv)
    barrier = pltpu.get_barrier_semaphore()
    for other in others:
        pl.semaphore_signal(barrier, inc=1, device_id=other, device_id_type=MESH)

    gain = gg[0].astype(F32) + gg[1].astype(F32)
    tc[c] = jnp.zeros((8, LANES), F32)
    for i in range(2):
        for h in range(2):
            tc[c, 2 * i + h : 2 * i + h + 1, :] = gain[i : i + 1, h * LANES : (h + 1) * LANES]

    k_in.wait()
    barrier_done = False
    k_cores = []
    for dx in (2, 1, 3, 0):
        xx = lax.rem(x + dx, NX)
        col = pl.ds(pl.multiple_of(xx * LANES, LANES), LANES)

        @pl.loop(0, 2)
        def _(zh):
            for zl in range(4):
                rows = pl.ds(pl.multiple_of((zh * 4 + zl) * ZR, 16), ZR)
                T[...] = kgv[0, rows, col].astype(F32) + kgv[1, rows, col].astype(F32)
                for k in range(NY * NC):
                    KK[k % NC, xx, k // NC, zh, R * zl : R * zl + R, :] = T[R * k : R * k + R, :]

        if not barrier_done:
            pl.semaphore_wait(barrier, len(others))
            barrier_done = True
        k_cores.append((xx, links.send(KK.at[oc, xx], RK.at[xx], sibling)))

    def chain_k():
        yield from scatter_ring(
            links, NX, x, lambda i: device(x=i),
            lambda i, part: KK.at[c, i, 2 * part : 2 * part + 2],
            lambda way, part, d: rKx.at[(1 - way) // 2, part, d - 1],
        )
        yield from scatter_direct(links, NY, y, lambda i: device(y=i), lambda i: KK.at[c, x, i], rKy)
        K3[...] = jnp.zeros_like(K3)
        for zz in range(NZ):
            K3[zz, 0:R, :] = KK[c, x, y, zz // 4, R * (zz % 4) : R * (zz % 4) + R, :]
        yield from scatter_direct(links, NZ, z, lambda i: device(z=i), lambda i: K3.at[i], rKz)

    def chain_b():
        yield from scatter_ring(
            links, NZ, z, lambda i: device(z=i),
            lambda i, part: PB.at[c, i, 2 * part : 2 * part + 2],
            lambda way, part, d: rBz.at[(1 - way) // 2, part, d - 1],
        )
        yield from scatter_direct(links, NY, y, lambda i: device(y=i), lambda i: PB.at[c, z, i], rBy)

    def chain_a():
        yield from scatter_ring(
            links, NY, y, lambda i: device(y=i),
            lambda i, part: PA.at[c, i, 4 * part : 4 * part + 4],
            lambda way, part, d: rAy.at[(1 - way) // 2, part, d - 1],
        )
        yield from scatter_direct(links, NZ, z, lambda i: device(z=i), lambda i: PA.at[c, y, i], rAz)

    for_k, for_b, for_a = chain_k(), chain_b(), chain_a()
    p_in.wait()
    for p in (1, 0):

        @pl.loop(0, NZ)
        def _(zz):
            rows = pl.ds(pl.multiple_of(zz * ZR, 16), ZR)
            for h in range(2):
                col = slice(h * LANES, (h + 1) * LANES)
                T[...] = pgv[0, p, rows, col].astype(F32) + pgv[1, p, rows, col].astype(F32)
                for k in range(NY * NC):
                    yy, cc = k // NC, k % NC
                    q = 2 * p + h
                    if q < 2:
                        PA[cc, yy, zz, R * q : R * q + R, :] = T[R * k : R * k + R, :]
                    elif q == 2:
                        PA[cc, yy, zz, 36:40, :] = T[R * k : R * k + 4, :]
                        PB[cc, zz, yy, 0:14, :] = T[R * k + 4 : R * k + R, :]
                    else:
                        PB[cc, zz, yy, 14:32, :] = T[R * k : R * k + R, :]

        if p == 1:
            b_core = links.send(PB.at[oc], RB, sibling)
            for xx, copy in k_cores:
                copy.wait_recv()
                KK[c, xx] = KK[c, xx] + RK[xx]
            next(for_k)

    a_core = links.send(PA.at[oc], RA, sibling)

    b_core.wait_recv()

    @pl.loop(0, NZ)
    def _(zz):
        PB[c, zz] = PB[c, zz] + RB[zz]

    next(for_b)
    next(for_k)
    a_core.wait_recv()

    @pl.loop(0, NY)
    def _(yy):
        PA[c, yy] = PA[c, yy] + RA[yy]

    next(for_a)
    for chain in (for_b, for_k, for_b, for_a, for_b, for_a, for_k, for_b, for_a, for_b, for_k):
        next(chain, None)

    S72[0:40, :] = PA[c, y, z]
    S72[40:72, :] = PB[c, z, y]
    p_sum, k_sum = S72[...], K3[z]
    squares = jnp.sum(p_sum * p_sum, axis=0, keepdims=True) + jnp.sum(k_sum * k_sum, axis=0, keepdims=True)
    tc[c, 4:5, :] = squares
    for slots, n, me, where in (
        (tc, NC, c, lambda i: device(c=i)),
        (tx, NX, x, lambda i: device(x=i)),
        (ty, NY, y, lambda i: device(y=i)),
        (tz, NZ, z, lambda i: device(z=i)),
    ):
        if slots is not tc:
            slots[me] = total
        copies = []
        for d in range(1, n):
            copies.append(links.send(slots.at[me], slots.at[me], where(lax.rem(me + d, n))))
        for copy in copies:
            copy.wait_recv()
        total = slots[0]
        for i in range(1, n):
            total = total + slots[i]
    tile_o[...] = total
    clip = clip_of(total)

    W96[...] = jnp.zeros_like(W96)
    for p in range(2):
        for h in range(2):
            q = 2 * p + h
            col = slice(h * LANES, (h + 1) * LANES)
            g = S72[R * q : R * q + R, :]
            psum_o[:, p, col] = g
            W96[R * q : R * q + R, :] = adamw_step(
                p_master[:, p, col], p_m[:, p, col], p_v[:, p, col], clip * g, decay_rate
            )[0]
    g = K3[z, 0:R, :]
    ksum_o[...] = g
    W96[72 : 72 + R, :] = adamw_step(k_master[...], k_m[...], k_v[...], clip * g, decay_rate)[0]
    G[c, z, y] = W96[...].astype(BF16)

    up_y, down_y = device(y=lax.rem(y + 1, NY)), device(y=lax.rem(y + NY - 1, NY))
    ahead, behind = lax.rem(y + 1, NY), lax.rem(y + NY - 1, NY)
    far = lax.rem(y + 2, NY)
    own = G.at[c, z, y]
    y_copies = [links.send(own, own, device(y=far)), links.send(own, own, up_y), links.send(own, own, down_y)]

    up_z, down_z = device(z=lax.rem(z + 1, NZ)), device(z=lax.rem(z + NZ - 1, NZ))
    order = (y, behind, ahead, far)

    def plane_moves(zz, yy, dev):
        ref = G.at[c, zz, yy]
        return links.send(ref, ref, dev)

    up, down, twin = {}, {}, {}
    for j, copy in enumerate((None, y_copies[1], y_copies[2], y_copies[0])):
        if copy is not None:
            copy.wait_recv()
        up[1, j] = plane_moves(z, order[j], up_z)
        down[1, j] = plane_moves(z, order[j], down_z)
    own_plane = G.at[c, z]
    twin[0, 0] = links.send(own_plane, own_plane, sibling)

    def unpack(zz):
        for k in range(NY * NC):
            block = G[k % NC, zz, k // NC].astype(F32)
            W96[...] = block
            for q in range(5):
                T5[q, R * k : R * k + R, :] = W96[R * q : R * q + R, :]
        for p in range(2):
            for h in range(2):
                pw_o[p, zz, :, h * LANES : (h + 1) * LANES] = T5[2 * p + h].astype(BF16)
        FK[x, zz] = T5[4].astype(BF16)

    up_x, down_x = device(x=lax.rem(x + 1, NX)), device(x=lax.rem(x + NX - 1, NX))
    over_x = device(x=lax.rem(x + 2, NX))
    x_first = {}

    def x_block(j):
        return lax.rem(z + (1 - 2 * c) * j - c + NZ, NZ)

    def x_start(j):
        ref = FK.at[x, x_block(j)]
        x_first[j] = tuple(links.send(ref, ref, to) for to in (over_x, up_x, down_x))

    for d in range(1, 5):
        below, above = lax.rem(z - d + NZ, NZ), lax.rem(z + d, NZ)
        if d < 4:
            for j in range(4):
                up[d, j].wait_recv()
                if d < 3:
                    up[d + 1, j] = plane_moves(below, order[j], up_z)
                elif j < 2:
                    up[4, j] = plane_moves(below, order[j], up_z)
                down[d, j].wait_recv()
                if d < 3:
                    down[d + 1, j] = plane_moves(above, order[j], down_z)
                elif j >= 2:
                    down[4, j] = plane_moves(above, order[j], down_z)
            for way, zz in ((0, below), (1, above)):
                ref = G.at[c, zz]
                twin[d, way] = links.send(ref, ref, sibling)
        else:
            for copy in (up[4, 0], up[4, 1], down[4, 2], down[4, 3]):
                copy.wait_recv()
            ref = G.at[c, above]
            twin[4, 0] = links.send(ref, ref, sibling)
        if d == 1:
            twin[0, 0].wait_recv()
            unpack(z)
        else:
            for way, zz in ((0, lax.rem(z - d + 1 + NZ, NZ)), (1, lax.rem(z + d - 1, NZ))):
                twin[d - 1, way].wait_recv()
                unpack(zz)
            x_start(d - 2)
    twin[4, 0].wait_recv()
    unpack(lax.rem(z + 4, NZ))
    x_start(3)

    x_behind, x_ahead, x_far = lax.rem(x + NX - 1, NX), lax.rem(x + 1, NX), lax.rem(x + 2, NX)
    x_twin = []
    for j in range(4):
        zz = x_block(j)
        for number, xx in ((1, x_behind), (2, x_ahead), (0, x_far)):
            x_first[j][number].wait_recv()
            ref = FK.at[xx, zz]
            x_twin.append(links.send(ref, ref, sibling))
    for copy in x_twin:
        copy.wait_recv()

    @pl.loop(0, NZ)
    def _(zz):
        for xx in range(NX):
            kw_o[zz, :, xx * LANES : (xx + 1) * LANES] = FK[xx, zz]

    assert len(links.started) <= N_COPIES
    links.finish()


def moments_kernel(
    psum, ksum, tile, pw, kw, p_master, p_m, p_v, k_master, k_m, k_v, gains, g_m, g_v,
    p_new, p_m_new, p_v_new, k_new, k_m_new, k_v_new, gains_new, g_m_new, g_v_new, pw_new, kw_new,
    pwv, kwv, in_sems, out_sems,
):
    pieces = []
    for i in range(4):
        p, half = i // 2, pl.ds(4 * (i % 2), 4)
        pieces.append((pw.at[p, half], pwv.at[p, half], pw_new.at[p, half]))
        pair = pl.ds(2 * i, 2)
        pieces.append((kw.at[pair], kwv.at[pair], kw_new.at[pair]))
    into = [pltpu.make_async_copy(src, mid, in_sems.at[i]) for i, (src, mid, _) in enumerate(pieces)]
    out = [pltpu.make_async_copy(mid, dst, out_sems.at[i]) for i, (_, mid, dst) in enumerate(pieces)]
    for copy in into:
        copy.start()
    for arrive, leave in zip(into, out):
        arrive.wait()
        leave.start()
    clip = clip_of(tile[...])
    scale = jnp.reshape(clip, (1, 1, 1))
    p_new[...], p_m_new[...], p_v_new[...] = adamw_step(
        p_master[...], p_m[...], p_v[...], scale * psum[...], decay_rate
    )
    k_new[...], k_m_new[...], k_v_new[...] = adamw_step(k_master[...], k_m[...], k_v[...], clip * ksum[...], decay_rate)
    for i in range(2):
        for h in range(2):
            col = slice(h * LANES, (h + 1) * LANES)
            row = slice(i, i + 1)
            g = tile[2 * i + h : 2 * i + h + 1, :]
            gains_new[row, col], g_m_new[row, col], g_v_new[row, col] = adamw_step(
                gains[row, col], g_m[row, col], g_v[row, col], clip * g, 0.0
            )
    for leave in out:
        leave.wait()


def shards(
    proj_grads,
    kv_grads,
    gain_grads,
    proj_master,
    proj_m,
    proj_v,
    kv_master,
    kv_m,
    kv_v,
    gains,
    gains_m,
    gains_v,
):
    proj_master, proj_m, proj_v = (jnp.transpose(a, (1, 0, 2)) for a in (proj_master, proj_m, proj_v))
    vmem, anywhere = pl.BlockSpec(memory_space=pltpu.VMEM), pl.BlockSpec(memory_space=pl.ANY)
    shape = jax.ShapeDtypeStruct
    scratch = [
        ((2, 2, 1152, 256), BF16), ((2, 1152, 512), BF16),
        ((NC, NY, NZ, 40, LANES), F32), ((NC, NZ, NY, 32, LANES), F32), ((NC, NX, NY, 2, 72, LANES), F32),
        ((NY, NZ, 40, LANES), F32), ((NZ, NY, 32, LANES), F32), ((NX, NY, 2, 72, LANES), F32),
        ((ZR, LANES), F32),
        ((2, 2, 2, 4, 40, LANES), F32), ((2, 2, 4, 2, 32, LANES), F32), ((2, 2, 2, 2, 2, 72, LANES), F32),
        ((NZ - 1, 40, LANES), F32), ((NY - 1, 32, LANES), F32), ((NY - 1, 2, 72, LANES), F32),
        ((NZ, 24, LANES), F32), ((NZ - 1, 24, LANES), F32),
        ((NC, 8, LANES), F32), ((NX, 8, LANES), F32), ((NY, 8, LANES), F32), ((NZ, 8, LANES), F32),
        ((72, LANES), F32), ((96, LANES), F32),
        ((NC, NZ, NY, 96, LANES), BF16), ((NX, NZ, ZR, LANES), BF16), ((5, ZR, LANES), F32),
    ]
    psum, ksum, tile, proj_weights, kv_weights = pl.pallas_call(
        step_kernel,
        name="reduce_update_gather",
        out_shape=[
            shape((R, 2, 256), F32),
            shape((R, LANES), F32),
            shape((8, LANES), F32),
            shape((2, NZ, ZR, 256), BF16),
            shape((NZ, ZR, 512), BF16),
        ],
        in_specs=[anywhere, anywhere] + [vmem] * 7,
        out_specs=[vmem] * 5,
        scratch_shapes=[pltpu.VMEM(s, d) for s, d in scratch]
        + [pltpu.SemaphoreType.DMA((N_COPIES,)), pltpu.SemaphoreType.DMA((N_COPIES,)), pltpu.SemaphoreType.DMA((2,))],
        compiler_params=pltpu.CompilerParams(
            collective_id=0, has_side_effects=True, vmem_limit_bytes=56 * 1024 * 1024
        ),
    )(proj_grads, kv_grads, gain_grads, proj_master, proj_m, proj_v, kv_master, kv_m, kv_v)
    state = (proj_master, proj_m, proj_v, kv_master, kv_m, kv_v, gains, gains_m, gains_v)
    new = pl.pallas_call(
        moments_kernel,
        name="moments",
        out_shape=[shape(a.shape, F32) for a in state] + [shape(a.shape, BF16) for a in (proj_weights, kv_weights)],
        in_specs=[vmem] * 3 + [anywhere] * 2 + [vmem] * 9,
        out_specs=[vmem] * 9 + [anywhere] * 2,
        scratch_shapes=[
            pltpu.VMEM(proj_weights.shape, BF16),
            pltpu.VMEM(kv_weights.shape, BF16),
            pltpu.SemaphoreType.DMA((8,)),
            pltpu.SemaphoreType.DMA((8,)),
        ],
    )(psum, ksum, tile, proj_weights, kv_weights, *state)
    return (
        *(jnp.transpose(a, (1, 0, 2)) for a in new[0:3]),
        new[9].reshape(2, 1152, 256),
        *new[3:6],
        new[10].reshape(1152, 512),
        *new[6:9],
    )


def solution(mesh):
    placed = (
        P("shard", None, None, "tensor"),
        P(("tensor", "shard"), None, None),
        P(("tensor", "shard"), None, None),
        P(None, "shard", "tensor"),
        P(None, "shard", "tensor"),
        P(None, "shard", "tensor"),
        P("shard", "tensor"),
        P("shard", "tensor"),
        P("shard", "tensor"),
        P(),
        P(),
        P(),
    )
    return jax.shard_map(
        shards,
        mesh=mesh,
        in_specs=placed,
        out_specs=(
            P(None, "shard", "tensor"),
            P(None, "shard", "tensor"),
            P(None, "shard", "tensor"),
            P(None, None, "tensor"),
            P("shard", "tensor"),
            P("shard", "tensor"),
            P("shard", "tensor"),
            P(),
            P(),
            P(),
            P(),
        ),
        check_vma=False,
    )
```

```python
import math

import jax
import jax.numpy as jnp
from jax import lax
from jax.experimental import pallas as pl
from jax.experimental.pallas import tpu as pltpu
from jax.sharding import PartitionSpec as P

PARAMS = 2949632
MESH = pl.DeviceIdType.MESH
F32, BF16 = jnp.float32, jnp.bfloat16

NZ, NY, NC, NX = 8, 4, 2, 4
R = 18
ZR = NY * NC * R
LANES = 128

beta_one = 0.9
beta_two = 0.95
learn_rate = 0.01
decay_rate = 0.1
epsilon = 1e-08
step_count = 10


def adamw_step(master, moment, second, update_grad, decay):
    moment_new = beta_one * moment + (1.0 - beta_one) * update_grad
    second_new = beta_two * second + (1.0 - beta_two) * update_grad * update_grad
    first_hat = moment_new / (1.0 - beta_one**step_count)
    second_hat = second_new / (1.0 - beta_two**step_count)
    master_new = master - learn_rate * (
        first_hat / (jnp.sqrt(second_hat) + epsilon) + decay * master
    )
    return (master_new, moment_new, second_new)


def clip_of(tile):
    row = lax.broadcasted_iota(jnp.int32, tile.shape, 0)
    terms = jnp.where(row < 4, tile * tile, jnp.where(row == 4, tile, 0.0))
    norm_square = jnp.sum(jnp.sum(terms, axis=0, keepdims=True), axis=1, keepdims=True)
    return jnp.minimum(1.0, math.sqrt(PARAMS) / jnp.sqrt(norm_square))


class Links:
    def __init__(self, send_sems, recv_sems, local_sems):
        self.send_sems, self.recv_sems, self.local_sems = send_sems, recv_sems, local_sems
        self.started, self.locals = [], 0

    def send(self, src, dst, device):
        number = len(self.started)
        copy = pltpu.make_async_remote_copy(
            src_ref=src,
            dst_ref=dst,
            send_sem=self.send_sems.at[number],
            recv_sem=self.recv_sems.at[number],
            device_id=device,
            device_id_type=MESH,
        )
        copy.start()
        self.started.append(copy)
        return copy

    def local(self, src, dst):
        copy = pltpu.make_async_copy(src, dst, self.local_sems.at[self.locals])
        self.locals += 1
        copy.start()
        return copy

    def finish(self):
        for copy in self.started:
            copy.wait_send()


N_COPIES = 176


def scatter_ring(links, n, pos, device, view, slot):
    half = n // 2
    copies = {}

    def step(way, part, d):
        dest = lax.rem(pos + way * d + n, n)
        copies[way, part, d] = links.send(view(dest, part), slot(way, part, d), device(lax.rem(pos + way + n, n)))

    def take(way, part, d):
        copies[way, part, d].wait_recv()
        dest = lax.rem(pos + way * (d - 1) + n, n)
        ref, got = view(dest, part), slot(way, part, d)
        ref[...] = ref[...] + got[...]

    for way in (1, -1):
        step(way, 0 if way == 1 else 1, half)
    if half > 1:
        for way in (1, -1):
            step(way, 1 if way == 1 else 0, half - 1)
    for d in range(half - 1, 0, -1):
        yield
        for way in (1, -1):
            lead = 0 if way == 1 else 1
            take(way, lead, d + 1)
            step(way, lead, d)
        if d < half - 1:
            for way in (1, -1):
                other = 1 if way == 1 else 0
                take(way, other, d + 1)
                step(way, other, d)
    yield
    for way in (1, -1):
        for part in (0, 1):
            if (way, part, 1) in copies:
                take(way, part, 1)


def scatter_direct(links, n, pos, device, view, slots):
    copies = {}
    for d in sorted(range(1, n), key=lambda d: -min(d, n - d)):
        dest = lax.rem(pos + d, n)
        copies[d] = links.send(view(dest), slots.at[d - 1], device(dest))
    yield
    own = view(pos)
    total = own[...]
    for d in sorted(range(1, n), key=lambda d: min(d, n - d)):
        copies[d].wait_recv()
        total = total + slots[d - 1]
    own[...] = total


def step_kernel(
    pg, kg, gg, p_master, p_m, p_v, k_master, k_m, k_v,
    psum_o, ksum_o, tile_o, pw_o, kw_o,
    pgv, kgv, PA, PB, KK, RA, RB, RK, T,
    rAy, rBz, rKx, rAz, rBy, rKy, K3, rKz,
    tc, txy, tz, S72, W96, G, FK, T5,
    send_sems, recv_sems, local_sems,
):
    shard, x = lax.axis_index("shard"), lax.axis_index("tensor")
    c = lax.rem(shard, NC)
    y = lax.rem(shard // NC, NY)
    z = shard // (NC * NY)
    oc = 1 - c

    def device(z=z, y=y, c=c, x=x):
        return {"shard": (z * NY + y) * NC + c, "tensor": x}

    links = Links(send_sems, recv_sems, local_sems)
    sibling = device(c=oc)
    others = [sibling]
    others += [device(x=lax.rem(x + d, NX)) for d in range(1, NX)]
    others += [device(y=lax.rem(y + d, NY)) for d in range(1, NY)]
    others += [device(z=lax.rem(z + d, NZ)) for d in range(1, NZ)]
    others += [device(x=lax.rem(x + i, NX), y=lax.rem(y + j, NY)) for i in range(1, NX) for j in range(1, NY)]

    k_in = links.local(kg, kgv)
    p_in = links.local(pg, pgv)
    barrier = pltpu.get_barrier_semaphore()
    for other in others:
        pl.semaphore_signal(barrier, inc=1, device_id=other, device_id_type=MESH)

    gain = gg[0].astype(F32) + gg[1].astype(F32)
    tc[c] = jnp.zeros((8, LANES), F32)
    for i in range(2):
        for h in range(2):
            tc[c, 2 * i + h : 2 * i + h + 1, :] = gain[i : i + 1, h * LANES : (h + 1) * LANES]

    k_in.wait()
    barrier_done = False
    k_cores = []
    for dx in (2, 1, 3, 0):
        xx = lax.rem(x + dx, NX)
        col = pl.ds(pl.multiple_of(xx * LANES, LANES), LANES)

        @pl.loop(0, 2)
        def _(zh):
            for zl in range(4):
                rows = pl.ds(pl.multiple_of((zh * 4 + zl) * ZR, 16), ZR)
                T[...] = kgv[0, rows, col].astype(F32) + kgv[1, rows, col].astype(F32)
                for k in range(NY * NC):
                    KK[k % NC, xx, k // NC, zh, R * zl : R * zl + R, :] = T[R * k : R * k + R, :]

        if not barrier_done:
            pl.semaphore_wait(barrier, len(others))
            barrier_done = True
        k_cores.append((xx, links.send(KK.at[oc, xx], RK.at[xx], sibling)))

    p_in.wait()
    for p in range(2):

        @pl.loop(0, NZ)
        def _(zz):
            rows = pl.ds(pl.multiple_of(zz * ZR, 16), ZR)
            for h in range(2):
                col = slice(h * LANES, (h + 1) * LANES)
                T[...] = pgv[0, p, rows, col].astype(F32) + pgv[1, p, rows, col].astype(F32)
                for k in range(NY * NC):
                    yy, cc = k // NC, k % NC
                    q = 2 * p + h
                    if q < 2:
                        PA[cc, yy, zz, R * q : R * q + R, :] = T[R * k : R * k + R, :]
                    elif q == 2:
                        PA[cc, yy, zz, 36:40, :] = T[R * k : R * k + 4, :]
                        PB[cc, zz, yy, 0:14, :] = T[R * k + 4 : R * k + R, :]
                    else:
                        PB[cc, zz, yy, 14:32, :] = T[R * k : R * k + R, :]

    b_core = links.send(PB.at[oc], RB, sibling)
    a_core = links.send(PA.at[oc], RA, sibling)

    for xx, copy in k_cores:
        copy.wait_recv()
        KK[c, xx] = KK[c, xx] + RK[xx]

    def chain_k():
        yield from scatter_ring(
            links, NX, x, lambda i: device(x=i),
            lambda i, part: KK.at[c, i, 2 * part : 2 * part + 2],
            lambda way, part, d: rKx.at[(1 - way) // 2, part, d - 1],
        )
        yield from scatter_direct(links, NY, y, lambda i: device(y=i), lambda i: KK.at[c, x, i], rKy)
        K3[...] = jnp.zeros_like(K3)
        for zz in range(NZ):
            K3[zz, 0:R, :] = KK[c, x, y, zz // 4, R * (zz % 4) : R * (zz % 4) + R, :]
        yield from scatter_direct(links, NZ, z, lambda i: device(z=i), lambda i: K3.at[i], rKz)

    def chain_b():
        yield from scatter_ring(
            links, NZ, z, lambda i: device(z=i),
            lambda i, part: PB.at[c, i, 2 * part : 2 * part + 2],
            lambda way, part, d: rBz.at[(1 - way) // 2, part, d - 1],
        )
        yield from scatter_direct(links, NY, y, lambda i: device(y=i), lambda i: PB.at[c, z, i], rBy)

    def chain_a():
        yield from scatter_ring(
            links, NY, y, lambda i: device(y=i),
            lambda i, part: PA.at[c, i, 4 * part : 4 * part + 4],
            lambda way, part, d: rAy.at[(1 - way) // 2, part, d - 1],
        )
        yield from scatter_direct(links, NZ, z, lambda i: device(z=i), lambda i: PA.at[c, y, i], rAz)

    for_k, for_b, for_a = chain_k(), chain_b(), chain_a()
    next(for_k)
    b_core.wait_recv()

    @pl.loop(0, NZ)
    def _(zz):
        PB[c, zz] = PB[c, zz] + RB[zz]

    next(for_b)
    a_core.wait_recv()

    @pl.loop(0, NY)
    def _(yy):
        PA[c, yy] = PA[c, yy] + RA[yy]

    next(for_a)
    for chain in (for_b, for_b, for_a, for_k, for_b, for_b, for_a, for_k, for_b, for_a, for_k, for_k):
        next(chain, None)

    S72[0:40, :] = PA[c, y, z]
    S72[40:72, :] = PB[c, z, y]
    p_sum, k_sum = S72[...], K3[z]
    squares = jnp.sum(p_sum * p_sum, axis=0, keepdims=True) + jnp.sum(k_sum * k_sum, axis=0, keepdims=True)
    tc[c, 4:5, :] = squares
    for slots, n, me, where in (
        (tc, NC, c, lambda i: device(c=i)),
        (txy, NX * NY, x * NY + y, lambda i: device(x=lax.div(i, NY), y=lax.rem(i, NY))),
        (tz, NZ, z, lambda i: device(z=i)),
    ):
        if slots is not tc:
            slots[me] = total
        copies = []
        for d in range(1, n):
            copies.append(links.send(slots.at[me], slots.at[me], where(lax.rem(me + d, n))))
        for copy in copies:
            copy.wait_recv()
        total = slots[0]
        for i in range(1, n):
            total = total + slots[i]
    tile_o[...] = total
    clip = clip_of(total)

    W96[...] = jnp.zeros_like(W96)
    for p in range(2):
        for h in range(2):
            q = 2 * p + h
            col = slice(h * LANES, (h + 1) * LANES)
            g = S72[R * q : R * q + R, :]
            psum_o[:, p, col] = g
            W96[R * q : R * q + R, :] = adamw_step(
                p_master[:, p, col], p_m[:, p, col], p_v[:, p, col], clip * g, decay_rate
            )[0]
    g = K3[z, 0:R, :]
    ksum_o[...] = g
    W96[72 : 72 + R, :] = adamw_step(k_master[...], k_m[...], k_v[...], clip * g, decay_rate)[0]
    G[c, z, y] = W96[...].astype(BF16)

    up_y, down_y = device(y=lax.rem(y + 1, NY)), device(y=lax.rem(y + NY - 1, NY))
    ahead, behind = lax.rem(y + 1, NY), lax.rem(y + NY - 1, NY)
    far = lax.rem(y + 2, NY)
    own = G.at[c, z, y]
    y_copies = [links.send(own, own, device(y=far)), links.send(own, own, up_y), links.send(own, own, down_y)]

    up_z, down_z = device(z=lax.rem(z + 1, NZ)), device(z=lax.rem(z + NZ - 1, NZ))
    order = (y, behind, ahead, far)

    def plane_moves(zz, yy, dev):
        ref = G.at[c, zz, yy]
        return links.send(ref, ref, dev)

    up, down, twin = {}, {}, {}
    for j, copy in enumerate((None, y_copies[1], y_copies[2], y_copies[0])):
        if copy is not None:
            copy.wait_recv()
        up[1, j] = plane_moves(z, order[j], up_z)
        down[1, j] = plane_moves(z, order[j], down_z)
    own_plane = G.at[c, z]
    twin[0, 0] = links.send(own_plane, own_plane, sibling)

    def unpack(zz):
        for k in range(NY * NC):
            block = G[k % NC, zz, k // NC].astype(F32)
            W96[...] = block
            for q in range(5):
                T5[q, R * k : R * k + R, :] = W96[R * q : R * q + R, :]
        for p in range(2):
            for h in range(2):
                pw_o[p, zz, :, h * LANES : (h + 1) * LANES] = T5[2 * p + h].astype(BF16)
        FK[x, zz] = T5[4].astype(BF16)

    up_x, down_x = device(x=lax.rem(x + 1, NX)), device(x=lax.rem(x + NX - 1, NX))
    over_x = device(x=lax.rem(x + 2, NX))
    x_first = {}

    def x_block(j):
        return lax.rem(z + (1 - 2 * c) * j - c + NZ, NZ)

    def x_start(j):
        ref = FK.at[x, x_block(j)]
        x_first[j] = tuple(links.send(ref, ref, to) for to in (over_x, up_x, down_x))

    for d in range(1, 5):
        below, above = lax.rem(z - d + NZ, NZ), lax.rem(z + d, NZ)
        if d < 4:
            for j in range(4):
                up[d, j].wait_recv()
                if d < 3:
                    up[d + 1, j] = plane_moves(below, order[j], up_z)
                elif j < 2:
                    up[4, j] = plane_moves(below, order[j], up_z)
                down[d, j].wait_recv()
                if d < 3:
                    down[d + 1, j] = plane_moves(above, order[j], down_z)
                elif j >= 2:
                    down[4, j] = plane_moves(above, order[j], down_z)
            for way, zz in ((0, below), (1, above)):
                ref = G.at[c, zz]
                twin[d, way] = links.send(ref, ref, sibling)
        else:
            for copy in (up[4, 0], up[4, 1], down[4, 2], down[4, 3]):
                copy.wait_recv()
            ref = G.at[c, above]
            twin[4, 0] = links.send(ref, ref, sibling)
        if d == 1:
            twin[0, 0].wait_recv()
            unpack(z)
        else:
            for way, zz in ((0, lax.rem(z - d + 1 + NZ, NZ)), (1, lax.rem(z + d - 1, NZ))):
                twin[d - 1, way].wait_recv()
                unpack(zz)
            x_start(d - 2)
    twin[4, 0].wait_recv()
    unpack(lax.rem(z + 4, NZ))
    x_start(3)

    x_behind, x_ahead, x_far = lax.rem(x + NX - 1, NX), lax.rem(x + 1, NX), lax.rem(x + 2, NX)
    x_twin = []
    for j in range(4):
        zz = x_block(j)
        for number, xx in ((1, x_behind), (2, x_ahead), (0, x_far)):
            x_first[j][number].wait_recv()
            ref = FK.at[xx, zz]
            x_twin.append(links.send(ref, ref, sibling))
    for copy in x_twin:
        copy.wait_recv()

    @pl.loop(0, NZ)
    def _(zz):
        for xx in range(NX):
            kw_o[zz, :, xx * LANES : (xx + 1) * LANES] = FK[xx, zz]

    assert len(links.started) <= N_COPIES
    links.finish()


def moments_kernel(
    psum, ksum, tile, pw, kw, p_master, p_m, p_v, k_master, k_m, k_v, gains, g_m, g_v,
    p_new, p_m_new, p_v_new, k_new, k_m_new, k_v_new, gains_new, g_m_new, g_v_new, pw_new, kw_new,
    pwv, kwv, in_sems, out_sems,
):
    pieces = []
    for i in range(4):
        p, half = i // 2, pl.ds(4 * (i % 2), 4)
        pieces.append((pw.at[p, half], pwv.at[p, half], pw_new.at[p, half]))
        pair = pl.ds(2 * i, 2)
        pieces.append((kw.at[pair], kwv.at[pair], kw_new.at[pair]))
    into = [pltpu.make_async_copy(src, mid, in_sems.at[i]) for i, (src, mid, _) in enumerate(pieces)]
    out = [pltpu.make_async_copy(mid, dst, out_sems.at[i]) for i, (_, mid, dst) in enumerate(pieces)]
    for copy in into:
        copy.start()
    for arrive, leave in zip(into, out):
        arrive.wait()
        leave.start()
    clip = clip_of(tile[...])
    scale = jnp.reshape(clip, (1, 1, 1))
    p_new[...], p_m_new[...], p_v_new[...] = adamw_step(
        p_master[...], p_m[...], p_v[...], scale * psum[...], decay_rate
    )
    k_new[...], k_m_new[...], k_v_new[...] = adamw_step(k_master[...], k_m[...], k_v[...], clip * ksum[...], decay_rate)
    for i in range(2):
        for h in range(2):
            col = slice(h * LANES, (h + 1) * LANES)
            row = slice(i, i + 1)
            g = tile[2 * i + h : 2 * i + h + 1, :]
            gains_new[row, col], g_m_new[row, col], g_v_new[row, col] = adamw_step(
                gains[row, col], g_m[row, col], g_v[row, col], clip * g, 0.0
            )
    for leave in out:
        leave.wait()


def shards(
    proj_grads,
    kv_grads,
    gain_grads,
    proj_master,
    proj_m,
    proj_v,
    kv_master,
    kv_m,
    kv_v,
    gains,
    gains_m,
    gains_v,
):
    proj_master, proj_m, proj_v = (jnp.transpose(a, (1, 0, 2)) for a in (proj_master, proj_m, proj_v))
    vmem, anywhere = pl.BlockSpec(memory_space=pltpu.VMEM), pl.BlockSpec(memory_space=pl.ANY)
    shape = jax.ShapeDtypeStruct
    scratch = [
        ((2, 2, 1152, 256), BF16), ((2, 1152, 512), BF16),
        ((NC, NY, NZ, 40, LANES), F32), ((NC, NZ, NY, 32, LANES), F32), ((NC, NX, NY, 2, 72, LANES), F32),
        ((NY, NZ, 40, LANES), F32), ((NZ, NY, 32, LANES), F32), ((NX, NY, 2, 72, LANES), F32),
        ((ZR, LANES), F32),
        ((2, 2, 2, 4, 40, LANES), F32), ((2, 2, 4, 2, 32, LANES), F32), ((2, 2, 2, 2, 2, 72, LANES), F32),
        ((NZ - 1, 40, LANES), F32), ((NY - 1, 32, LANES), F32), ((NY - 1, 2, 72, LANES), F32),
        ((NZ, 24, LANES), F32), ((NZ - 1, 24, LANES), F32),
        ((NC, 8, LANES), F32), ((NX * NY, 8, LANES), F32), ((NZ, 8, LANES), F32),
        ((72, LANES), F32), ((96, LANES), F32),
        ((NC, NZ, NY, 96, LANES), BF16), ((NX, NZ, ZR, LANES), BF16), ((5, ZR, LANES), F32),
    ]
    psum, ksum, tile, proj_weights, kv_weights = pl.pallas_call(
        step_kernel,
        name="reduce_update_gather",
        out_shape=[
            shape((R, 2, 256), F32),
            shape((R, LANES), F32),
            shape((8, LANES), F32),
            shape((2, NZ, ZR, 256), BF16),
            shape((NZ, ZR, 512), BF16),
        ],
        in_specs=[anywhere, anywhere] + [vmem] * 7,
        out_specs=[vmem] * 5,
        scratch_shapes=[pltpu.VMEM(s, d) for s, d in scratch]
        + [pltpu.SemaphoreType.DMA((N_COPIES,)), pltpu.SemaphoreType.DMA((N_COPIES,)), pltpu.SemaphoreType.DMA((2,))],
        compiler_params=pltpu.CompilerParams(
            collective_id=0, has_side_effects=True, vmem_limit_bytes=56 * 1024 * 1024
        ),
    )(proj_grads, kv_grads, gain_grads, proj_master, proj_m, proj_v, kv_master, kv_m, kv_v)
    state = (proj_master, proj_m, proj_v, kv_master, kv_m, kv_v, gains, gains_m, gains_v)
    new = pl.pallas_call(
        moments_kernel,
        name="moments",
        out_shape=[shape(a.shape, F32) for a in state] + [shape(a.shape, BF16) for a in (proj_weights, kv_weights)],
        in_specs=[vmem] * 3 + [anywhere] * 2 + [vmem] * 9,
        out_specs=[vmem] * 9 + [anywhere] * 2,
        scratch_shapes=[
            pltpu.VMEM(proj_weights.shape, BF16),
            pltpu.VMEM(kv_weights.shape, BF16),
            pltpu.SemaphoreType.DMA((8,)),
            pltpu.SemaphoreType.DMA((8,)),
        ],
    )(psum, ksum, tile, proj_weights, kv_weights, *state)
    return (
        *(jnp.transpose(a, (1, 0, 2)) for a in new[0:3]),
        new[9].reshape(2, 1152, 256),
        *new[3:6],
        new[10].reshape(1152, 512),
        *new[6:9],
    )


def solution(mesh):
    placed = (
        P("shard", None, None, "tensor"),
        P(("tensor", "shard"), None, None),
        P(("tensor", "shard"), None, None),
        P(None, "shard", "tensor"),
        P(None, "shard", "tensor"),
        P(None, "shard", "tensor"),
        P("shard", "tensor"),
        P("shard", "tensor"),
        P("shard", "tensor"),
        P(),
        P(),
        P(),
    )
    return jax.shard_map(
        shards,
        mesh=mesh,
        in_specs=placed,
        out_specs=(
            P(None, "shard", "tensor"),
            P(None, "shard", "tensor"),
            P(None, "shard", "tensor"),
            P(None, None, "tensor"),
            P("shard", "tensor"),
            P("shard", "tensor"),
            P("shard", "tensor"),
            P(),
            P(),
            P(),
            P(),
        ),
        check_vma=False,
    )
```
